32 devices in a mesh: sec: 2 (over core), req: 4 (over z), head: 4 (over y, x).
Axes of the slice: x: 2, y: 2, z: 4, core: 2. Of those that a mesh axis runs over, the one named last changes fastest.
Arguments:
- queries: bfloat16 [32, 32, 4096], P(('sec', 'req'), None, 'head'), as said below
- tree_keys: bfloat16 [32, 32, 512], P(('sec', 'req'), None, 'head'), may hold values from -4 to 4
- tree_values: bfloat16 [32, 32, 512], P(('sec', 'req'), None, 'head'), may hold values from -4 to 4
- cache_keys: bfloat16 [32, 4, 4096, 128], P(('sec', 'req'), 'head'), as said below
- cache_values: bfloat16 [32, 4, 4096, 128], P(('sec', 'req'), 'head'), may hold values from -4 to 4
- cache_lengths: int32 [32], P(('sec', 'req')), may hold values from 1024 to 4096
- tree_parents: int32 [32, 32], P(('sec', 'req')), may hold values from 0 to 30, as said below
- out_weight: bfloat16 [4096, 2048], P('head'), may hold values from -0.09375 to 0.09375
- hidden: bfloat16 [1024, 2048], P(('sec', 'req', 'head')), may hold values from -0.1796875 to 0.1796875
- norm_gain: float32 [2048], replicated, may hold values from 0.1 to 1.9
- expert_ids: int32 [1024, 8], P(('sec', 'req', 'head')), may hold values from 0 to 31, all different within a row; in each aligned block of 32 rows (0 to 31, 32 to 63, ...) at most 16 rows name the same one
- route_weights: float32 [1024, 8], P(('sec', 'req', 'head')), may hold values from 0.05 to 0.25
- expert_gate_up: bfloat16 [32, 2048, 1536], P(('sec', 'req', 'head')), may hold values from -0.125 to 0.125
- expert_down: bfloat16 [32, 768, 2048], P(('sec', 'req', 'head')), may hold values from -0.21875 to 0.21875
Outputs:
- layer_out: bfloat16 [1024, 2048], P(('sec', 'req', 'head'))
The draws below stay inside these ranges and needn't reach their ends.
Inputs may be any that keep to these rules, and one draw needn't show every extreme that they name: `queries`: values lie within -4.5 to 4.5. `cache_keys`: values lie within -4.5 to 4.5. tree_parents[r, i] < i for i >= 1, and tree_parents[r, 0] = 0. `expert_ids`: each row names 8 different experts. Among the 32 rows of one device (aligned blocks of rows), no expert is named more than 16 times, a bound that some block reaches.
All inputs are finite; a program needn't handle non-finite values.
Results may differ from the reference program's by a relative error of at most 0.02.
Values may be sent and summed in bfloat16 or wider, within the bound.
A program may use at most 128 MiB of HBM per device.

```python
import math
import jax
import jax.numpy as jnp
import numpy as np
from jax import lax

D = 2048
HEADS = 32
KVH = 4
HD = 128
FFE = 768
TOPK = 8
TREE = 32
CACHE = 4096
EXPERTS = 32
REQUESTS = 32
TOKENS = 1024
TOK_SHARD = 32
CAP = 16


def draw_queries(key, part):
    drawn = 1.5 * jax.random.truncated_normal(jax.random.fold_in(key, 21), -3.0, 3.0, (REQUESTS, TREE, KVH, HEADS // KVH, HD), jnp.float32)
    return drawn.reshape(REQUESTS, TREE, HEADS * HD).astype(jnp.bfloat16)


def draw_cache_keys(key, part):
    drawn = jax.random.truncated_normal(jax.random.fold_in(key, 31), -3.0, 3.0, (REQUESTS, KVH, CACHE, HD), jnp.float32)
    return drawn.astype(jnp.bfloat16)


def draw_tree_parents(key, part):
    limits = jnp.maximum(jnp.arange(TREE, dtype=jnp.int32), 1)
    return jax.random.randint(jax.random.fold_in(key, 41), (REQUESTS, TREE), 0, limits[None, :], dtype=jnp.int32)


def touch_ends(result, stream_key, low, largest):
    place = [jax.random.randint(jax.random.fold_in(stream_key, axis), (), 0, length) for axis, length in enumerate(result.shape)]
    longest = result.shape.index(max(result.shape))
    beside = place[:longest] + [(place[longest] + 1) % result.shape[longest]] + place[longest + 1:]
    return result.at[tuple(place)].set(low).at[tuple(beside)].set(largest)


def shard_levels(stream_key, extent, cuts, smallest, high):
    def one(dim, parts):
        draws = jax.random.uniform(jax.random.fold_in(jax.random.fold_in(stream_key, 6), dim), (parts,), jnp.float32, smallest / len(cuts), high / len(cuts))
        return jnp.repeat(jnp.exp(draws), extent[dim] // parts).reshape((-1,) + (1,) * (len(extent) - dim - 1))

    loudness = one(*cuts[0])
    for cut in cuts[1:]:
        loudness = loudness * one(*cut)
    return loudness


def deal_out(own_key, own, number, rows, count, top, bound, skew):
    order = jax.random.permutation(own_key, count)
    crowded, ordinary = portions_of(count, rows * top, bound, skew, True), portions_of(count, rows * top, bound, skew, False)
    places = jnp.arange(count)

    def named(tallies, rotation):
        used = int((tallies > 0).sum())
        fixed = max(1, used // 4)
        moved = fixed + (places - fixed + rotation * (used - fixed)) % max(1, count - fixed)
        return jnp.zeros((count,), jnp.int32).at[order[jnp.where(places < fixed, places, moved)]].set(jnp.asarray(tallies, jnp.int32))

    tallies = jnp.where(number % 4 == 0, named(crowded, number // 4), named(ordinary, number - number // 4 - 1))
    mixed = jax.random.permutation(jax.random.fold_in(own, 3), count)
    source_of, taker = mixed[0:count // 2 * 2:2], mixed[1:count // 2 * 2:2]
    room = jnp.minimum(tallies[source_of] - 1, bound - tallies[taker]) // 2
    room = jnp.where((source_of == order[0]) | (taker == order[0]) | (tallies[taker] == 0), 0, jnp.maximum(room, 0))
    moved = jax.random.randint(jax.random.fold_in(own, 4), (count // 2,), 0, 1 << 20) % (room + 1)
    tallies = tallies.at[source_of].add(-moved).at[taker].add(moved)
    members = jnp.searchsorted(jnp.cumsum(tallies), jnp.arange(rows * top), side="right").astype(jnp.int32)
    grid = members.reshape(top, rows).T
    grid = grid[jax.random.permutation(jax.random.fold_in(own, 1), rows)]
    rotation = jax.random.randint(jax.random.fold_in(own, 2), (rows, 1), 0, top)
    return jnp.take_along_axis(grid, (jnp.arange(top)[None, :] + rotation) % top, axis=1)


def portions_of(number_of, total, reach, skew, full):
    loads = [(1 << 20) // math.isqrt(grade ** skew) + 1 for grade in range(1, number_of + 1)]
    largest = reach if full else min(reach, max(-(-total // number_of), total * loads[0] // sum(loads)))
    least = 1 if total - largest >= number_of - 1 else 0
    given, rest = [largest] + [least] * (number_of - 1), total - largest - least * (number_of - 1)
    while rest > 0:
        movable = [i for i in range(1, number_of) if given[i] < largest] or [i for i in range(1, number_of) if given[i] < reach]
        whole, budget = sum([loads[i] for i in movable]), rest
        for i in movable:
            extra = min(reach - given[i], max(1, budget * loads[i] // whole), rest)
            given[i] = given[i] + extra
            rest = rest - extra
    return np.array(given)


def scatter_about(own_key, dims, deviation, reach, cuts=(), kind=jnp.bfloat16):
    array = jax.random.normal(own_key, dims, jnp.float32) * deviation
    if len(cuts) > 0:
        array = shard_levels(own_key, dims, cuts, -0.22, 0.18) * array
    return jnp.clip(array, min=-reach, max=reach).astype(kind)


def setup_inputs(seed: int = 0) -> dict:
    splits = jax.random.split(jax.random.key(seed), 15)
    queries = draw_queries(jax.random.fold_in(splits[14], 71), 0)
    tree_keys = scatter_about(splits[1], (REQUESTS, TREE, KVH * HD), 1.0, 4.0, ((0, 8), (2, 4)))
    tree_values = scatter_about(splits[2], (REQUESTS, TREE, KVH * HD), 1.0, 4.0, ((0, 8), (2, 4)))
    cache_keys = draw_cache_keys(jax.random.fold_in(splits[14], 71), 0)
    cache_values = scatter_about(splits[4], (REQUESTS, KVH, CACHE, HD), 1.0, 4.0, ((0, 8), (1, 4)))
    cache_lengths = touch_ends(jax.random.randint(splits[5], (REQUESTS,), CACHE // 4, CACHE + 1), jax.random.fold_in(splits[5], 1), CACHE // 4, CACHE).astype(jnp.int32)
    tree_parents = draw_tree_parents(jax.random.fold_in(splits[14], 71), 0)
    out_weight = scatter_about(splits[7], (HEADS * HD, D), (HEADS * HD) ** -0.5, 0.09375, ((0, 4),))
    hidden = scatter_about(splits[8], (TOKENS, D), 0.03, 0.1796875, ((0, 32),))
    norm_gain = jnp.clip(1.0 + 0.18 * jax.random.normal(splits[9], (D,), jnp.float32), 0.1, 1.9)
    expert_ids_keys = jax.random.split(jax.random.fold_in(splits[10], 1), TOKENS // TOK_SHARD)
    expert_ids_turns = jax.random.permutation(jax.random.fold_in(splits[10], 3), TOKENS // TOK_SHARD)
    expert_ids = jax.vmap(lambda own, number: deal_out(jax.random.fold_in(splits[10], 2), own, number, TOK_SHARD, EXPERTS, TOPK, CAP, 2))(expert_ids_keys, expert_ids_turns).reshape((TOKENS, TOPK))
    route_weights = jnp.clip(0.05 + 0.2 * jax.random.uniform(splits[11], (TOKENS, TOPK), jnp.float32) ** shard_levels(splits[11], (TOKENS, TOPK), ((0, 32),), -0.2, 0.2), 0.05, 0.25)
    expert_gate_up = scatter_about(splits[12], (EXPERTS, D, 2 * FFE), D ** -0.5, 0.125, ((0, 32),))
    expert_down = scatter_about(splits[13], (EXPERTS, FFE, D), FFE ** -0.5, 0.21875, ((0, 32),))
    return {"queries": queries, "tree_keys": tree_keys, "tree_values": tree_values, "cache_keys": cache_keys, "cache_values": cache_values, "cache_lengths": cache_lengths, "tree_parents": tree_parents, "out_weight": out_weight, "hidden": hidden, "norm_gain": norm_gain, "expert_ids": expert_ids, "route_weights": route_weights, "expert_gate_up": expert_gate_up, "expert_down": expert_down}


def ancestors(parents):
    length = parents.shape[-1]
    labels = jnp.arange(length, dtype=jnp.int32)
    linked = (parents[..., :, None] == labels).astype(jnp.float32)
    closure = jnp.minimum(linked + jnp.eye(length, dtype=jnp.float32), 1.0)
    for repeat in range(max(1, (length - 1).bit_length())):
        closure = jnp.minimum(jnp.einsum('rij,rjk->rik', closure, closure), 1.0)
    return closure

def attend_request(packed):
    query_rows, tree_keys, tree_values, cache_keys, cache_values, cache_length, closure = packed
    tree_len = query_rows.shape[0]
    kv_heads, cache_len, head_dim = cache_keys.shape
    groups = query_rows.shape[1] // (kv_heads * head_dim)
    query_split = query_rows.astype(jnp.float32).reshape(tree_len, kv_heads, groups, head_dim)
    tree_keyed = tree_keys.astype(jnp.float32).reshape(tree_len, kv_heads, head_dim)
    tree_valued = tree_values.astype(jnp.float32).reshape(tree_len, kv_heads, head_dim)
    score_scale = head_dim ** (-0.5)
    cache_scores = jnp.einsum('skgd,kcd->kgsc', query_split, cache_keys.astype(jnp.float32)) * score_scale
    tree_scores = jnp.einsum('skgd,tkd->kgst', query_split, tree_keyed) * score_scale
    cache_valid = jnp.arange(cache_len, dtype=jnp.int32) < cache_length
    cache_scores = jnp.where(cache_valid, cache_scores, -1e+30)
    tree_scores = jnp.where(closure > 0.5, tree_scores, -1e+30)
    highest = jnp.maximum(lax.optimization_barrier(jnp.max(cache_scores, -1)), lax.optimization_barrier(jnp.max(tree_scores, -1)))[..., None]
    cache_exp = jnp.exp(cache_scores - highest)
    tree_exp = jnp.exp(tree_scores - highest)
    denominator = lax.optimization_barrier(jnp.sum(cache_exp, -1, keepdims=True)) + lax.optimization_barrier(jnp.sum(tree_exp, -1, keepdims=True))
    cache_prob = lax.optimization_barrier((cache_exp / denominator).astype(jnp.bfloat16)).astype(jnp.float32)
    tree_prob = lax.optimization_barrier((tree_exp / denominator).astype(jnp.bfloat16)).astype(jnp.float32)
    attended = jnp.einsum('kgsc,kcd->skgd', cache_prob, cache_values.astype(jnp.float32))
    attended = attended + jnp.einsum('kgst,tkd->skgd', tree_prob, tree_valued)
    return attended.reshape(tree_len, query_rows.shape[1]).astype(jnp.bfloat16)

def expert_apply(packed):
    expert_rows, gate_up, down_proj = packed
    mixed = jnp.dot(expert_rows, gate_up, preferred_element_type=jnp.float32)
    activated = (jax.nn.silu(mixed[:, :FFE]) * mixed[:, FFE:]).astype(jnp.bfloat16)
    return jnp.dot(activated, down_proj, preferred_element_type=jnp.float32).astype(jnp.bfloat16)

def reference(queries, tree_keys, tree_values, cache_keys, cache_values, cache_lengths, tree_parents, out_weight, hidden, norm_gain, expert_ids, route_weights, expert_gate_up, expert_down):
    closure = ancestors(tree_parents)
    attended = lax.map(attend_request, (queries, tree_keys, tree_values, cache_keys, cache_values, cache_lengths, closure))
    attended = attended.reshape(TOKENS, HEADS * HD)
    resid = hidden.astype(jnp.float32) + jnp.dot(attended, out_weight, preferred_element_type=jnp.float32)
    normed = (resid * lax.rsqrt(lax.optimization_barrier(jnp.mean(resid * resid, -1, keepdims=True)) + 1e-06) * norm_gain).astype(jnp.bfloat16)
    flat_ids = expert_ids.reshape(-1).astype(jnp.int32)
    bucket_size = TOKENS // TOK_SHARD * CAP
    onehot = (flat_ids[:, None] == jnp.arange(EXPERTS, dtype=jnp.int32)[None, :]).astype(jnp.int32)
    ranking = lax.optimization_barrier(jnp.sum((jnp.cumsum(onehot, 0) - onehot) * onehot, -1)).astype(jnp.int32)
    slot_index = (flat_ids * bucket_size + ranking).astype(jnp.int32)
    owners = (jnp.arange(TOKENS * TOPK, dtype=jnp.int32) // TOPK).astype(jnp.int32)
    token_of = jnp.zeros((EXPERTS * bucket_size,), jnp.int32).at[slot_index].set(owners)
    expert_rows = normed[token_of].reshape(EXPERTS, bucket_size, D)
    outputs = lax.map(expert_apply, (expert_rows, expert_gate_up, expert_down)).reshape(EXPERTS * bucket_size, D)
    picked = outputs[slot_index].reshape(TOKENS, TOPK, D).astype(jnp.float32)
    expert_sum = jnp.einsum('tk,tkd->td', route_weights, picked)
    return (resid + expert_sum).astype(jnp.bfloat16)
```

```python
import functools
import math

import jax
import jax.numpy as jnp
from jax import lax
from jax.experimental import pallas as pl
from jax.experimental.pallas import tpu as pltpu
from jax.sharding import PartitionSpec as P

F32 = jnp.float32
BF16 = jnp.bfloat16
NEG = -1e30
CHUNK = 512
LANES = 128


def dot_nt(a, b):
    return lax.dot_general(a, b, (((1,), (1,)), ((), ())), preferred_element_type=F32)


def dot_nn(a, b):
    return jnp.dot(a, b, preferred_element_type=F32)


def attend_kernel(
    len_ref, q_ref, tk_ref, tv_ref, par_ref, ck_ref, cv_ref, wo_hbm, out_ref,
    attended, m_ref, l_ref, acc_ref, wo_ref, wo_sem,
):
    r = pl.program_id(0)
    last = pl.num_programs(0) - 1
    weights = pltpu.make_async_copy(wo_hbm, wo_ref, wo_sem)

    @pl.when(r == 0)
    def _():
        weights.start()

    tree, width = q_ref.shape[1:]
    hd = ck_ref.shape[3]
    cache = ck_ref.shape[2]
    chunk = min(CHUNK, cache)
    groups = width // hd
    scale = hd ** (-0.5) * math.log2(math.e)
    q = q_ref[0]
    rows = jnp.concatenate([q[:, g * hd : (g + 1) * hd] for g in range(groups)], axis=0)

    down = lax.broadcasted_iota(jnp.int32, (tree, tree), 0)
    across = lax.broadcasted_iota(jnp.int32, (tree, tree), 1)
    eye = (down == across).astype(F32)
    linked_t = (jnp.broadcast_to(par_ref[0], (tree, tree)) == down).astype(F32)
    closure = jnp.minimum(dot_nt(eye.astype(BF16), linked_t.astype(BF16)) + eye, 1.0)
    for _ in range(max(1, (tree - 1).bit_length())):
        half = closure.astype(BF16)
        closure = jnp.minimum(dot_nn(half, half), 1.0)
    admitted = jnp.concatenate([closure] * groups, axis=0)

    scores = jnp.where(admitted > 0.5, dot_nt(rows, tk_ref[0]) * scale, NEG)
    highest = jnp.max(scores, -1, keepdims=True)
    probs = jnp.exp2(scores - highest)
    m_ref[...] = jnp.broadcast_to(highest, m_ref.shape)
    l_ref[...] = jnp.broadcast_to(jnp.sum(probs, -1, keepdims=True), l_ref.shape)
    acc_ref[...] = dot_nn(probs.astype(BF16), tv_ref[0])

    length = len_ref[r]

    def step(start, masked):
        start = pl.multiple_of(start, chunk)
        s = dot_nt(rows, ck_ref[0, 0, pl.ds(start, chunk), :]) * scale
        if masked:
            place = lax.broadcasted_iota(jnp.int32, s.shape, 1)
            s = jnp.where(place < length - start, s, NEG)
        before = m_ref[:, :1]
        now = jnp.maximum(before, jnp.max(s, -1, keepdims=True))
        p = jnp.exp2(s - now)
        fade = jnp.exp2(before - now)
        l_ref[...] = l_ref[...] * fade + jnp.sum(p, -1, keepdims=True)
        acc_ref[...] = acc_ref[...] * fade + dot_nn(
            p.astype(BF16), cv_ref[0, 0, pl.ds(start, chunk), :]
        )
        m_ref[...] = jnp.broadcast_to(now, m_ref.shape)

    whole = length // chunk

    @pl.loop(0, whole)
    def _(i):
        step(i * chunk, False)

    @pl.when(whole * chunk < length)
    def _():
        step(whole * chunk, True)

    o = (acc_ref[...] / l_ref[:, :1]).astype(BF16)
    for g in range(groups):
        attended[r, :, g * hd : (g + 1) * hd] = o[g * tree : (g + 1) * tree]

    @pl.when(r == last)
    def _():
        weights.wait()
        a = attended[...].reshape(-1, width)
        out_ref[...] = dot_nn(a, wo_ref[...]).astype(BF16)


def attend(queries, tree_keys, tree_values, cache_keys, cache_values, lengths, parents, out_weight):
    req, tree, width = queries.shape
    cache, hd = cache_keys.shape[2:]
    assert cache_keys.shape[1] == 1
    model = out_weight.shape[1]
    rows = tree * (width // hd)
    grid_spec = pltpu.PrefetchScalarGridSpec(
        num_scalar_prefetch=1,
        grid=(req,),
        in_specs=[
            pl.BlockSpec((1, tree, width), lambda r, n: (r, 0, 0)),
            pl.BlockSpec((1, tree, hd), lambda r, n: (r, 0, 0)),
            pl.BlockSpec((1, tree, hd), lambda r, n: (r, 0, 0)),
            pl.BlockSpec((1, 1, tree), lambda r, n: (r, 0, 0)),
            pl.BlockSpec((1, 1, cache, hd), lambda r, n: (r, 0, 0, 0)),
            pl.BlockSpec((1, 1, cache, hd), lambda r, n: (r, 0, 0, 0)),
            pl.BlockSpec(memory_space=pl.ANY),
        ],
        out_specs=pl.BlockSpec((req * tree, model), lambda r, n: (0, 0)),
        scratch_shapes=[
            pltpu.VMEM((req, tree, width), BF16),
            pltpu.VMEM((rows, LANES), F32),
            pltpu.VMEM((rows, LANES), F32),
            pltpu.VMEM((rows, hd), F32),
            pltpu.VMEM(out_weight.shape, BF16),
            pltpu.SemaphoreType.DMA,
        ],
    )
    return pl.pallas_call(
        attend_kernel,
        grid_spec=grid_spec,
        out_shape=jax.ShapeDtypeStruct((req * tree, model), BF16),
        compiler_params=pltpu.CompilerParams(
            dimension_semantics=("arbitrary",), vmem_limit_bytes=48 << 20
        ),
    )(lengths, queries, tree_keys, tree_values, parents.reshape(req, 1, tree), cache_keys,
      cache_values, out_weight)


def copy_count(z_n, y_n, x_n):
    gather = 2 * (z_n - 1) + z_n * (x_n * y_n - 1) * 2 + 2 * z_n
    back = 2 * z_n + 2 * z_n * (y_n - 1 + x_n - 1) + 2 * (z_n - 1)
    return (y_n * x_n - 1) + gather + back


def expert_kernel(
    dims, part_ref, hid_ref, gain_ref, ids_ref, rw_ref, gu_hbm, dn_hbm, out_ref,
    head_in, bank, sums, pair_in, first_in, second_in, z_in, resid_ref, gu, dn,
    send, recv, load_sem,
):
    z_n, y_n, x_n = dims
    h_n = y_n * x_n
    s = lax.axis_index("sec")
    z = lax.axis_index("req")
    h = lax.axis_index("head")
    y = h // x_n
    x = h % x_n
    tok, model = hid_ref.shape
    half = model // 2
    mine = (s * z_n + z) * h_n + h

    def to_head(k):
        return {"head": lax.rem(h + k, h_n)}

    def to_z(k):
        return {"req": lax.rem(z + k, z_n)}

    def to_yx(dy, dx):
        return {"head": lax.rem(y + dy, y_n) * x_n + lax.rem(x + dx, x_n)}

    partner = {"sec": 1 - s}
    barrier = pltpu.get_barrier_semaphore()
    peers = [to_head(k) for k in range(1, h_n)] + [to_z(k) for k in range(1, z_n)] + [partner]
    for peer in peers:
        pl.semaphore_signal(
            barrier, inc=1, device_id=peer, device_id_type=pl.DeviceIdType.MESH
        )
    load_gu = pltpu.make_async_copy(gu_hbm.at[0], gu, load_sem.at[0])
    load_dn = pltpu.make_async_copy(dn_hbm.at[0], dn, load_sem.at[1])
    load_gu.start()
    load_dn.start()
    pl.semaphore_wait(barrier, len(peers))

    made = []

    def push(src, dst, peer):
        k = len(made)
        c = pltpu.make_async_remote_copy(
            src_ref=src, dst_ref=dst, send_sem=send.at[k], recv_sem=recv.at[k],
            device_id=peer, device_id_type=pl.DeviceIdType.MESH,
        )
        made.append(c)
        c.start()
        return c

    arrivals = []
    for k in range(1, h_n):
        row = pl.multiple_of(lax.rem(h + k, h_n) * tok, tok)
        arrivals.append(push(part_ref.at[pl.ds(row, tok), :], head_in.at[k - 1], to_head(k)))
    lanes = bank.shape[-1] - half
    labels = lax.broadcasted_iota(jnp.int32, (tok, lanes), 1)
    dense = jnp.zeros((tok, lanes), F32)
    for k in range(ids_ref.shape[1]):
        dense = dense + jnp.where(ids_ref[:, k : k + 1] == labels, rw_ref[:, k : k + 1], 0.0)
    high = dense.astype(BF16)
    low = (dense - high.astype(F32)).astype(BF16)
    own_row = pl.multiple_of(h * tok, tok)
    resid = hid_ref[...].astype(F32) + part_ref[pl.ds(own_row, tok), :].astype(F32)
    for k in range(1, h_n):
        arrivals[k - 1].wait_recv()
        resid = resid + head_in[k - 1].astype(F32)
    resid_ref[...] = resid
    normed = (
        resid * lax.rsqrt(jnp.mean(resid * resid, -1, keepdims=True) + 1e-06) * gain_ref[...]
    ).astype(BF16)
    for f, extra in ((0, high), (1, low)):
        bank[0, f, 0, 0, 0, :, :half] = normed[:, f * half : (f + 1) * half]
        bank[0, f, 0, 0, 0, :, half:] = extra

    got = {}

    def gather(f, dz, dy, dx, src, peer):
        got[f, dz, dy, dx] = push(
            bank.at[(0, f, dz) + src], bank.at[0, f, dz, dy, dx], peer
        )

    for dz in range(1, z_n):
        for f in range(2):
            got[f, dz, 0, 0] = push(bank.at[0, f, 0, 0, 0], bank.at[0, f, dz, 0, 0], to_z(dz))

    def stage_a(dz):
        for f in range(2):
            if dz:
                got[f, dz, 0, 0].wait_recv()
            for dx in range(1, x_n):
                gather(f, dz, 0, dx, (0, 0), to_yx(0, dx)) if f == 0 else None
            for dy in range(1, y_n):
                gather(f, dz, dy, 0, (0, 0), to_yx(dy, 0)) if f == 1 else None
        for dy in range(1, y_n):
            gather(0, dz, dy, 0, (0, 0), to_yx(dy, 0))
        for dx in range(1, x_n):
            gather(1, dz, 0, dx, (0, 0), to_yx(0, dx))

    def stage_b(dz):
        for dx in range(1, x_n):
            got[0, dz, 0, dx].wait_recv()
            for dy in range(1, y_n):
                gather(0, dz, dy, dx, (0, dx), to_yx(dy, 0))
        for dy in range(1, y_n):
            got[1, dz, dy, 0].wait_recv()
            for dx in range(1, x_n):
                gather(1, dz, dy, dx, (dy, 0), to_yx(0, dx))

    crossed = {}

    def stage_c(dz):
        for f in range(2):
            for dy in range(y_n):
                for dx in range(x_n):
                    seen = (dy == 0 and dx == 0) or (f == 0 and dy == 0) or (f == 1 and dx == 0)
                    if not seen:
                        got[f, dz, dy, dx].wait_recv()
            crossed[f, dz] = push(bank.at[0, f, dz], bank.at[1, f, dz], partner)

    count = 2 * h_n * tok
    apart = 1 if h_n * tok <= 128 else y_n

    def experts(dz):
        for f in range(2):
            crossed[f, dz].wait_recv()
        pick = lax.broadcasted_iota(jnp.int32, (1, lanes), 1) == mine
        for part in range(apart):
            ys = slice(part * (y_n // apart), (part + 1) * (y_n // apart))
            left = bank[:, 0, dz, ys].reshape(count // apart, half + lanes)
            right = bank[:, 1, dz, ys].reshape(count // apart, half + lanes)
            named = left[:, half:].astype(F32) + right[:, half:].astype(F32)
            weight = jnp.sum(jnp.where(pick, named, 0.0), -1, keepdims=True)
            mixed = dot_nn(left[:, :half], gu[:half]) + dot_nn(right[:, :half], gu[half:])
            hidden = mixed.shape[1] // 2
            gate = mixed[:, :hidden]
            active = (gate / (1.0 + jnp.exp(-gate)) * mixed[:, hidden:]).astype(BF16)
            result = jnp.where(weight > 0.0, dot_nn(active, dn[...]) * weight, 0.0).astype(BF16)
            shaped = result.reshape(2, y_n // apart, x_n, tok, model)
            for f in range(2):
                sums[f, dz, ys] = shaped[0, ..., f * half : (f + 1) * half]
                bank[1, f, dz, ys, :, :, :half] = shaped[1, ..., f * half : (f + 1) * half]

    paired, firsts, seconds, ends = {}, {}, {}, {}

    def back_pair(dz):
        for f in range(2):
            paired[f, dz] = push(
                bank.at[1, f, dz, :, :, :, pl.ds(0, half)], pair_in.at[f, dz], partner
            )

    def back_first(dz):
        for f in range(2):
            paired[f, dz].wait_recv()
            sums[f, dz] = (sums[f, dz].astype(F32) + pair_in[f, dz].astype(F32)).astype(BF16)
            if f == 0:
                for dy in range(1, y_n):
                    firsts[f, dz, dy] = push(
                        sums.at[f, dz, dy], first_in.at[f, dz, dy - 1], to_yx(y_n - dy, 0)
                    )
            else:
                for dx in range(1, x_n):
                    firsts[f, dz, dx] = push(
                        sums.at[f, dz, :, dx], first_in.at[f, dz, dx - 1], to_yx(0, x_n - dx)
                    )

    def back_second(dz):
        for f in range(2):
            total = sums[f, dz, 0] if f == 0 else sums[f, dz, :, 0]
            total = total.astype(F32)
            for d in range(1, y_n if f == 0 else x_n):
                firsts[f, dz, d].wait_recv()
                total = total + first_in[f, dz, d - 1].astype(F32)
            if f == 0:
                sums[f, dz, 0] = total.astype(BF16)
                for dx in range(1, x_n):
                    seconds[f, dz, dx] = push(
                        sums.at[f, dz, 0, dx], second_in.at[f, dz, dx - 1], to_yx(0, x_n - dx)
                    )
            else:
                sums[f, dz, :, 0] = total.astype(BF16)
                for dy in range(1, y_n):
                    seconds[f, dz, dy] = push(
                        sums.at[f, dz, dy, 0], second_in.at[f, dz, dy - 1], to_yx(y_n - dy, 0)
                    )

    def back_end(dz):
        for f in range(2):
            total = sums[f, dz, 0, 0].astype(F32)
            for d in range(1, x_n if f == 0 else y_n):
                seconds[f, dz, d].wait_recv()
                total = total + second_in[f, dz, d - 1].astype(F32)
            if dz:
                sums[f, dz, 0, 0] = total.astype(BF16)
                ends[f, dz] = push(sums.at[f, dz, 0, 0], z_in.at[f, dz - 1], to_z(z_n - dz))
            else:
                cols = slice(f * half, (f + 1) * half)
                resid_ref[:, cols] = resid_ref[:, cols] + total

    steps = []
    for i in range(z_n + 4):
        for stage, lag in ((stage_a, 0), (stage_b, 1), (stage_c, 2)):
            if 0 <= i - lag < z_n:
                stage(i - lag)
        if i == 2:
            load_gu.wait()
            load_dn.wait()
        dz = i - 3
        if 0 <= dz < z_n:
            experts(dz)
            back_pair(dz)
            steps.append(dz)
        for stage, lag in ((back_end, 3), (back_second, 2), (back_first, 1)):
            at = len(steps) - 1 - lag if i < z_n + 3 else -1
            if steps and 0 <= at < z_n:
                stage(at)
    for at in range(z_n):
        for stage, lag in ((back_end, 3), (back_second, 2), (back_first, 1)):
            todo = at + z_n - lag
            if todo < z_n:
                stage(todo)
    for f in range(2):
        cols = slice(f * half, (f + 1) * half)
        total = resid_ref[:, cols]
        for dz in range(1, z_n):
            ends[f, dz].wait_recv()
            total = total + z_in[f, dz - 1].astype(F32)
        out_ref[:, cols] = total.astype(BF16)
    for c in made:
        c.wait_send()
    assert len(made) == copy_count(*dims)


def expert_layer(dims, partial, hidden, gain, ids, route, gate_up, down):
    z_n, y_n, x_n = dims
    tok, model = hidden.shape
    half = model // 2
    experts = gate_up.shape[0] * 2 * z_n * y_n * x_n
    assert gate_up.shape[0] == 1 and partial.shape[0] == y_n * x_n * tok
    lanes = -(-experts // LANES) * LANES
    most = max(y_n, x_n)
    copies = copy_count(*dims)
    vmem = pl.BlockSpec(memory_space=pltpu.VMEM)
    return pl.pallas_call(
        functools.partial(expert_kernel, dims),
        out_shape=jax.ShapeDtypeStruct((tok, model), BF16),
        in_specs=[vmem] * 5 + [pl.BlockSpec(memory_space=pl.ANY)] * 2,
        out_specs=vmem,
        scratch_shapes=[
            pltpu.VMEM((y_n * x_n - 1, tok, model), BF16),
            pltpu.VMEM((2, 2, z_n, y_n, x_n, tok, half + lanes), BF16),
            pltpu.VMEM((2, z_n, y_n, x_n, tok, half), BF16),
            pltpu.VMEM((2, z_n, y_n, x_n, tok, half), BF16),
            pltpu.VMEM((2, z_n, most - 1, most, tok, half), BF16),
            pltpu.VMEM((2, z_n, most - 1, tok, half), BF16),
            pltpu.VMEM((2, z_n - 1, tok, half), BF16),
            pltpu.VMEM((tok, model), F32),
            pltpu.VMEM(gate_up.shape[1:], BF16),
            pltpu.VMEM(down.shape[1:], BF16),
            pltpu.SemaphoreType.DMA((copies,)),
            pltpu.SemaphoreType.DMA((copies,)),
            pltpu.SemaphoreType.DMA((2,)),
        ],
        compiler_params=pltpu.CompilerParams(
            collective_id=0, has_side_effects=True, vmem_limit_bytes=67043328
        ),
    )(partial, hidden, gain.reshape(1, -1), ids, route, gate_up, down)


def per_device(
    dims, queries, tree_keys, tree_values, cache_keys, cache_values, cache_lengths, tree_parents,
    out_weight, hidden, norm_gain, expert_ids, route_weights, expert_gate_up, expert_down,
):
    partial = attend(
        queries, tree_keys, tree_values, cache_keys, cache_values, cache_lengths, tree_parents,
        out_weight,
    )
    return expert_layer(
        dims, partial, hidden, norm_gain, expert_ids, route_weights, expert_gate_up, expert_down
    )


def solution(mesh):
    heads = mesh.shape["head"]
    x_n = math.isqrt(heads)
    while heads % x_n:
        x_n -= 1
    assert mesh.shape["sec"] == 2
    dims = (mesh.shape["req"], heads // x_n, x_n)
    tokens = ("sec", "req", "head")
    in_specs = (
        P(("sec", "req"), None, "head"),
        P(("sec", "req"), None, "head"),
        P(("sec", "req"), None, "head"),
        P(("sec", "req"), "head", None, None),
        P(("sec", "req"), "head", None, None),
        P(("sec", "req")),
        P(("sec", "req"), None),
        P("head", None),
        P(tokens, None),
        P(),
        P(tokens, None),
        P(tokens, None),
        P(tokens, None, None),
        P(tokens, None, None),
    )
    return jax.shard_map(
        functools.partial(per_device, dims), mesh=mesh, in_specs=in_specs,
        out_specs=P(tokens, None), check_vma=False,
    )
```

```python
import functools
import math

import jax
import jax.numpy as jnp
from jax import lax
from jax.experimental import pallas as pl
from jax.experimental.pallas import tpu as pltpu
from jax.sharding import PartitionSpec as P

F32 = jnp.float32
BF16 = jnp.bfloat16
NEG = -1e30
CHUNKS = (2048, 512)
LANES = 128


def dot_nt(a, b):
    return lax.dot_general(a, b, (((1,), (1,)), ((), ())), preferred_element_type=F32)


def dot_nn(a, b):
    return jnp.dot(a, b, preferred_element_type=F32)


def attend_kernel(
    len_ref, q_ref, tk_ref, tv_ref, par_ref, ck_ref, cv_ref, wo_hbm, out_ref,
    attended, m_ref, l_ref, acc_ref, wo_ref, wo_sem,
):
    r = pl.program_id(0)
    last = pl.num_programs(0) - 1
    weights = pltpu.make_async_copy(wo_hbm, wo_ref, wo_sem)

    @pl.when(r == 0)
    def _():
        weights.start()

    tree, width = q_ref.shape[1:]
    hd = ck_ref.shape[3]
    cache = ck_ref.shape[2]
    groups = width // hd
    scale = hd ** (-0.5) * math.log2(math.e)
    q = q_ref[0]
    rows = jnp.concatenate([q[:, g * hd : (g + 1) * hd] for g in range(groups)], axis=0)

    down = lax.broadcasted_iota(jnp.int32, (tree, tree), 0)
    across = lax.broadcasted_iota(jnp.int32, (tree, tree), 1)
    eye = (down == across).astype(F32)
    linked_t = (jnp.broadcast_to(par_ref[0], (tree, tree)) == down).astype(F32)
    closure = jnp.minimum(dot_nt(eye.astype(BF16), linked_t.astype(BF16)) + eye, 1.0)
    for _ in range(max(1, (tree - 1).bit_length())):
        half = closure.astype(BF16)
        closure = jnp.minimum(dot_nn(half, half), 1.0)
    admitted = jnp.concatenate([closure] * groups, axis=0)

    scores = jnp.where(admitted > 0.5, dot_nt(rows, tk_ref[0]) * scale, NEG)
    highest = jnp.max(scores, -1, keepdims=True)
    probs = jnp.exp2(scores - highest)
    m_ref[...] = jnp.broadcast_to(highest, m_ref.shape)
    l_ref[...] = jnp.broadcast_to(jnp.sum(probs, -1, keepdims=True), l_ref.shape)
    acc_ref[...] = dot_nn(probs.astype(BF16), tv_ref[0])

    length = len_ref[r]

    def step(start, chunk, masked):
        start = pl.multiple_of(start, chunk)
        s = dot_nt(rows, ck_ref[0, 0, pl.ds(start, chunk), :]) * scale
        if masked:
            place = lax.broadcasted_iota(jnp.int32, s.shape, 1)
            s = jnp.where(place < length - start, s, NEG)
        before = m_ref[:, :1]
        now = jnp.maximum(before, jnp.max(s, -1, keepdims=True))
        p = jnp.exp2(s - now)
        fade = jnp.exp2(before - now)
        l_ref[...] = l_ref[...] * fade + jnp.sum(p, -1, keepdims=True)
        acc_ref[...] = acc_ref[...] * fade + dot_nn(
            p.astype(BF16), cv_ref[0, 0, pl.ds(start, chunk), :]
        )
        m_ref[...] = jnp.broadcast_to(now, m_ref.shape)

    done = 0
    for chunk in CHUNKS:
        assert cache % chunk == 0
        upto = length // chunk

        @pl.loop(done // chunk, upto)
        def _(i, chunk=chunk):
            step(i * chunk, chunk, False)

        done = upto * chunk

    @pl.when(done < length)
    def _():
        step(done, CHUNKS[-1], True)

    o = (acc_ref[...] / l_ref[:, :1]).astype(BF16)
    for g in range(groups):
        attended[r, :, g * hd : (g + 1) * hd] = o[g * tree : (g + 1) * tree]

    @pl.when(r == last)
    def _():
        weights.wait()
        a = attended[...].reshape(-1, width)
        out_ref[...] = dot_nn(a, wo_ref[...]).astype(BF16)


def attend(queries, tree_keys, tree_values, cache_keys, cache_values, lengths, parents, out_weight):
    req, tree, width = queries.shape
    cache, hd = cache_keys.shape[2:]
    assert cache_keys.shape[1] == 1
    model = out_weight.shape[1]
    rows = tree * (width // hd)
    grid_spec = pltpu.PrefetchScalarGridSpec(
        num_scalar_prefetch=1,
        grid=(req,),
        in_specs=[
            pl.BlockSpec((1, tree, width), lambda r, n: (r, 0, 0)),
            pl.BlockSpec((1, tree, hd), lambda r, n: (r, 0, 0)),
            pl.BlockSpec((1, tree, hd), lambda r, n: (r, 0, 0)),
            pl.BlockSpec((1, 1, tree), lambda r, n: (r, 0, 0)),
            pl.BlockSpec((1, 1, cache, hd), lambda r, n: (r, 0, 0, 0)),
            pl.BlockSpec((1, 1, cache, hd), lambda r, n: (r, 0, 0, 0)),
            pl.BlockSpec(memory_space=pl.ANY),
        ],
        out_specs=pl.BlockSpec((req * tree, model), lambda r, n: (0, 0)),
        scratch_shapes=[
            pltpu.VMEM((req, tree, width), BF16),
            pltpu.VMEM((rows, LANES), F32),
            pltpu.VMEM((rows, LANES), F32),
            pltpu.VMEM((rows, hd), F32),
            pltpu.VMEM(out_weight.shape, BF16),
            pltpu.SemaphoreType.DMA,
        ],
    )
    return pl.pallas_call(
        attend_kernel,
        grid_spec=grid_spec,
        out_shape=jax.ShapeDtypeStruct((req * tree, model), BF16),
        compiler_params=pltpu.CompilerParams(
            dimension_semantics=("arbitrary",), vmem_limit_bytes=67043328
        ),
    )(lengths, queries, tree_keys, tree_values, parents.reshape(req, 1, tree), cache_keys,
      cache_values, out_weight)


def copy_count(z_n, y_n, x_n):
    gather = 2 * (z_n - 1) + z_n * (x_n * y_n - 1) * 2 + 2 * z_n
    back = 2 * z_n + 2 * z_n * (y_n - 1 + x_n - 1) + 2 * (z_n - 1)
    return (y_n * x_n - 1) + gather + back


def expert_kernel(
    dims, part_ref, hid_ref, gain_ref, ids_ref, rw_ref, gu_hbm, dn_hbm, out_ref,
    head_in, bank, sums, pair_in, first_in, second_in, z_in, resid_ref, gu, dn,
    send, recv, load_sem,
):
    z_n, y_n, x_n = dims
    h_n = y_n * x_n
    s = lax.axis_index("sec")
    z = lax.axis_index("req")
    h = lax.axis_index("head")
    y = h // x_n
    x = h % x_n
    tok, model = hid_ref.shape
    half = model // 2
    mine = (s * z_n + z) * h_n + h

    def to_head(k):
        return {"head": lax.rem(h + k, h_n)}

    def to_z(k):
        return {"req": lax.rem(z + k, z_n)}

    def to_yx(dy, dx):
        return {"head": lax.rem(y + dy, y_n) * x_n + lax.rem(x + dx, x_n)}

    partner = {"sec": 1 - s}
    barrier = pltpu.get_barrier_semaphore()
    peers = [to_head(k) for k in range(1, h_n)] + [to_z(k) for k in range(1, z_n)] + [partner]
    for peer in peers:
        pl.semaphore_signal(
            barrier, inc=1, device_id=peer, device_id_type=pl.DeviceIdType.MESH
        )
    load_gu = pltpu.make_async_copy(gu_hbm.at[0], gu, load_sem.at[0])
    load_dn = pltpu.make_async_copy(dn_hbm.at[0], dn, load_sem.at[1])
    load_gu.start()
    load_dn.start()
    pl.semaphore_wait(barrier, len(peers))

    made = []

    def push(src, dst, peer):
        k = len(made)
        c = pltpu.make_async_remote_copy(
            src_ref=src, dst_ref=dst, send_sem=send.at[k], recv_sem=recv.at[k],
            device_id=peer, device_id_type=pl.DeviceIdType.MESH,
        )
        made.append(c)
        c.start()
        return c

    arrivals = []
    for k in range(1, h_n):
        row = pl.multiple_of(lax.rem(h + k, h_n) * tok, tok)
        arrivals.append(push(part_ref.at[pl.ds(row, tok), :], head_in.at[k - 1], to_head(k)))
    lanes = bank.shape[-1] - half
    labels = lax.broadcasted_iota(jnp.int32, (lanes, tok), 0)
    dense = jnp.zeros((lanes, tok), F32)
    for k in range(ids_ref.shape[0]):
        dense = dense + jnp.where(ids_ref[k : k + 1, :] == labels, rw_ref[k : k + 1, :], 0.0)
    high = dense.astype(BF16)
    low = (dense - high.astype(F32)).astype(BF16)
    eye = (
        lax.broadcasted_iota(jnp.int32, (tok, tok), 0)
        == lax.broadcasted_iota(jnp.int32, (tok, tok), 1)
    ).astype(F32).astype(BF16)
    high = dot_nt(eye, high).astype(BF16)
    low = dot_nt(eye, low).astype(BF16)
    own_row = pl.multiple_of(h * tok, tok)
    resid = hid_ref[...].astype(F32) + part_ref[pl.ds(own_row, tok), :].astype(F32)
    for k in range(1, h_n):
        arrivals[k - 1].wait_recv()
        resid = resid + head_in[k - 1].astype(F32)
    resid_ref[...] = resid
    normed = (
        resid * lax.rsqrt(jnp.mean(resid * resid, -1, keepdims=True) + 1e-06) * gain_ref[...]
    ).astype(BF16)
    for f, extra in ((0, high), (1, low)):
        bank[0, f, 0, 0, 0, :, :half] = normed[:, f * half : (f + 1) * half]
        bank[0, f, 0, 0, 0, :, half:] = extra

    got = {}

    def gather(f, dz, dy, dx, src, peer):
        got[f, dz, dy, dx] = push(
            bank.at[(0, f, dz) + src], bank.at[0, f, dz, dy, dx], peer
        )

    for dz in range(1, z_n):
        for f in range(2):
            got[f, dz, 0, 0] = push(bank.at[0, f, 0, 0, 0], bank.at[0, f, dz, 0, 0], to_z(dz))

    def stage_a(dz):
        for f in range(2):
            if dz:
                got[f, dz, 0, 0].wait_recv()
            for dx in range(1, x_n):
                gather(f, dz, 0, dx, (0, 0), to_yx(0, dx)) if f == 0 else None
            for dy in range(1, y_n):
                gather(f, dz, dy, 0, (0, 0), to_yx(dy, 0)) if f == 1 else None
        for dy in range(1, y_n):
            gather(0, dz, dy, 0, (0, 0), to_yx(dy, 0))
        for dx in range(1, x_n):
            gather(1, dz, 0, dx, (0, 0), to_yx(0, dx))

    def stage_b(dz):
        for dx in range(1, x_n):
            got[0, dz, 0, dx].wait_recv()
            for dy in range(1, y_n):
                gather(0, dz, dy, dx, (0, dx), to_yx(dy, 0))
        for dy in range(1, y_n):
            got[1, dz, dy, 0].wait_recv()
            for dx in range(1, x_n):
                gather(1, dz, dy, dx, (dy, 0), to_yx(0, dx))

    crossed = {}

    def stage_c(dz):
        for f in range(2):
            for dy in range(y_n):
                for dx in range(x_n):
                    seen = (dy == 0 and dx == 0) or (f == 0 and dy == 0) or (f == 1 and dx == 0)
                    if not seen:
                        got[f, dz, dy, dx].wait_recv()
            crossed[f, dz] = push(bank.at[0, f, dz], bank.at[1, f, dz], partner)

    count = 2 * h_n * tok
    apart = 1 if h_n * tok <= 128 else y_n

    def experts(dz):
        for f in range(2):
            crossed[f, dz].wait_recv()
        pick = lax.broadcasted_iota(jnp.int32, (1, lanes), 1) == mine
        for part in range(apart):
            ys = slice(part * (y_n // apart), (part + 1) * (y_n // apart))
            left = bank[:, 0, dz, ys].reshape(count // apart, half + lanes)
            right = bank[:, 1, dz, ys].reshape(count // apart, half + lanes)
            named = left[:, half:].astype(F32) + right[:, half:].astype(F32)
            weight = jnp.sum(jnp.where(pick, named, 0.0), -1, keepdims=True)
            mixed = dot_nn(left[:, :half], gu[:half]) + dot_nn(right[:, :half], gu[half:])
            hidden = mixed.shape[1] // 2
            gate = mixed[:, :hidden]
            active = (gate / (1.0 + jnp.exp(-gate)) * mixed[:, hidden:]).astype(BF16)
            result = jnp.where(weight > 0.0, dot_nn(active, dn[...]) * weight, 0.0).astype(BF16)
            shaped = result.reshape(2, y_n // apart, x_n, tok, model)
            for f in range(2):
                sums[f, dz, ys] = shaped[0, ..., f * half : (f + 1) * half]
                bank[1, f, dz, ys, :, :, :half] = shaped[1, ..., f * half : (f + 1) * half]

    paired, firsts, seconds, ends = {}, {}, {}, {}

    def back_pair(dz):
        for f in range(2):
            paired[f, dz] = push(
                bank.at[1, f, dz, :, :, :, pl.ds(0, half)], pair_in.at[f, dz], partner
            )

    def back_first(dz):
        for f in range(2):
            paired[f, dz].wait_recv()
            sums[f, dz] = (sums[f, dz].astype(F32) + pair_in[f, dz].astype(F32)).astype(BF16)
            if f == 0:
                for dy in range(1, y_n):
                    firsts[f, dz, dy] = push(
                        sums.at[f, dz, dy], first_in.at[f, dz, dy - 1], to_yx(y_n - dy, 0)
                    )
            else:
                for dx in range(1, x_n):
                    firsts[f, dz, dx] = push(
                        sums.at[f, dz, :, dx], first_in.at[f, dz, dx - 1], to_yx(0, x_n - dx)
                    )

    def back_second(dz):
        for f in range(2):
            total = sums[f, dz, 0] if f == 0 else sums[f, dz, :, 0]
            total = total.astype(F32)
            for d in range(1, y_n if f == 0 else x_n):
                firsts[f, dz, d].wait_recv()
                total = total + first_in[f, dz, d - 1].astype(F32)
            if f == 0:
                sums[f, dz, 0] = total.astype(BF16)
                for dx in range(1, x_n):
                    seconds[f, dz, dx] = push(
                        sums.at[f, dz, 0, dx], second_in.at[f, dz, dx - 1], to_yx(0, x_n - dx)
                    )
            else:
                sums[f, dz, :, 0] = total.astype(BF16)
                for dy in range(1, y_n):
                    seconds[f, dz, dy] = push(
                        sums.at[f, dz, dy, 0], second_in.at[f, dz, dy - 1], to_yx(y_n - dy, 0)
                    )

    def back_end(dz):
        for f in range(2):
            total = sums[f, dz, 0, 0].astype(F32)
            for d in range(1, x_n if f == 0 else y_n):
                seconds[f, dz, d].wait_recv()
                total = total + second_in[f, dz, d - 1].astype(F32)
            if dz:
                sums[f, dz, 0, 0] = total.astype(BF16)
                ends[f, dz] = push(sums.at[f, dz, 0, 0], z_in.at[f, dz - 1], to_z(z_n - dz))
            else:
                cols = slice(f * half, (f + 1) * half)
                resid_ref[:, cols] = resid_ref[:, cols] + total

    order = list(range(1, z_n)) + [0]

    def back(j):
        for stage, lag in ((back_end, 3), (back_second, 2), (back_first, 1)):
            if 0 <= j - lag < z_n:
                stage(order[j - lag])

    ran = 0
    for i in range(z_n + 2):
        for stage, lag in ((stage_a, 0), (stage_b, 1), (stage_c, 2)):
            if 0 <= i - lag < z_n:
                stage(i - lag)
        if i == 2:
            load_gu.wait()
            load_dn.wait()
        while ran < z_n and (i == z_n + 1 or order[ran] <= i - 2 and order[ran] > 0):
            experts(order[ran])
            back_pair(order[ran])
            back(ran)
            ran += 1
    for j in range(z_n, z_n + 3):
        back(j)
    for f in range(2):
        cols = slice(f * half, (f + 1) * half)
        total = resid_ref[:, cols]
        for dz in range(1, z_n):
            ends[f, dz].wait_recv()
            total = total + z_in[f, dz - 1].astype(F32)
        out_ref[:, cols] = total.astype(BF16)
    for c in made:
        c.wait_send()
    assert len(made) == copy_count(*dims)


def expert_layer(dims, partial, hidden, gain, ids, route, gate_up, down):
    z_n, y_n, x_n = dims
    tok, model = hidden.shape
    half = model // 2
    experts = gate_up.shape[0] * 2 * z_n * y_n * x_n
    assert gate_up.shape[0] == 1 and partial.shape[0] == y_n * x_n * tok
    lanes = -(-experts // LANES) * LANES
    most = max(y_n, x_n)
    copies = copy_count(*dims)
    vmem = pl.BlockSpec(memory_space=pltpu.VMEM)
    return pl.pallas_call(
        functools.partial(expert_kernel, dims),
        out_shape=jax.ShapeDtypeStruct((tok, model), BF16),
        in_specs=[vmem] * 5 + [pl.BlockSpec(memory_space=pl.ANY)] * 2,
        out_specs=vmem,
        scratch_shapes=[
            pltpu.VMEM((y_n * x_n - 1, tok, model), BF16),
            pltpu.VMEM((2, 2, z_n, y_n, x_n, tok, half + lanes), BF16),
            pltpu.VMEM((2, z_n, y_n, x_n, tok, half), BF16),
            pltpu.VMEM((2, z_n, y_n, x_n, tok, half), BF16),
            pltpu.VMEM((2, z_n, most - 1, most, tok, half), BF16),
            pltpu.VMEM((2, z_n, most - 1, tok, half), BF16),
            pltpu.VMEM((2, z_n - 1, tok, half), BF16),
            pltpu.VMEM((tok, model), F32),
            pltpu.VMEM(gate_up.shape[1:], BF16),
            pltpu.VMEM(down.shape[1:], BF16),
            pltpu.SemaphoreType.DMA((copies,)),
            pltpu.SemaphoreType.DMA((copies,)),
            pltpu.SemaphoreType.DMA((2,)),
        ],
        compiler_params=pltpu.CompilerParams(
            collective_id=0, has_side_effects=True, vmem_limit_bytes=67043328
        ),
    )(partial, hidden, gain.reshape(1, -1), ids.T, route.T, gate_up, down)


def per_device(
    dims, queries, tree_keys, tree_values, cache_keys, cache_values, cache_lengths, tree_parents,
    out_weight, hidden, norm_gain, expert_ids, route_weights, expert_gate_up, expert_down,
):
    partial = attend(
        queries, tree_keys, tree_values, cache_keys, cache_values, cache_lengths, tree_parents,
        out_weight,
    )
    return expert_layer(
        dims, partial, hidden, norm_gain, expert_ids, route_weights, expert_gate_up, expert_down
    )


def solution(mesh):
    heads = mesh.shape["head"]
    x_n = math.isqrt(heads)
    while heads % x_n:
        x_n -= 1
    assert mesh.shape["sec"] == 2
    dims = (mesh.shape["req"], heads // x_n, x_n)
    tokens = ("sec", "req", "head")
    in_specs = (
        P(("sec", "req"), None, "head"),
        P(("sec", "req"), None, "head"),
        P(("sec", "req"), None, "head"),
        P(("sec", "req"), "head", None, None),
        P(("sec", "req"), "head", None, None),
        P(("sec", "req")),
        P(("sec", "req"), None),
        P("head", None),
        P(tokens, None),
        P(),
        P(tokens, None),
        P(tokens, None),
        P(tokens, None, None),
        P(tokens, None, None),
    )
    return jax.shard_map(
        functools.partial(per_device, dims), mesh=mesh, in_specs=in_specs,
        out_specs=P(tokens, None), check_vma=False,
    )
```

```python
import functools
import math

import jax
import jax.numpy as jnp
from jax import lax
from jax.experimental import pallas as pl
from jax.experimental.pallas import tpu as pltpu
from jax.sharding import PartitionSpec as P

F32 = jnp.float32
BF16 = jnp.bfloat16
NEG = -1e30
CHUNKS = (2048, 512)
LANES = 128


def dot_nt(a, b):
    return lax.dot_general(a, b, (((1,), (1,)), ((), ())), preferred_element_type=F32)


def dot_nn(a, b):
    return jnp.dot(a, b, preferred_element_type=F32)


def attend_kernel(
    len_ref, q_ref, tk_ref, tv_ref, par_ref, ck_ref, cv_ref, wo_hbm, out_ref,
    attended, m_ref, l_ref, acc_ref, wo_ref, wo_sem,
):
    r = pl.program_id(0)
    last = pl.num_programs(0) - 1
    weights = pltpu.make_async_copy(wo_hbm, wo_ref, wo_sem)

    @pl.when(r == 0)
    def _():
        weights.start()

    tree, width = q_ref.shape[1:]
    hd = ck_ref.shape[3]
    cache = ck_ref.shape[2]
    groups = width // hd
    scale = hd ** (-0.5) * math.log2(math.e)
    q = q_ref[0]
    rows = jnp.concatenate([q[:, g * hd : (g + 1) * hd] for g in range(groups)], axis=0)

    down = lax.broadcasted_iota(jnp.int32, (tree, tree), 0)
    across = lax.broadcasted_iota(jnp.int32, (tree, tree), 1)
    eye = (down == across).astype(F32)
    linked_t = (jnp.broadcast_to(par_ref[0], (tree, tree)) == down).astype(F32)
    closure = jnp.minimum(dot_nt(eye.astype(BF16), linked_t.astype(BF16)) + eye, 1.0)
    for _ in range(max(1, (tree - 1).bit_length())):
        half = closure.astype(BF16)
        closure = jnp.minimum(dot_nn(half, half), 1.0)
    admitted = jnp.concatenate([closure] * groups, axis=0)

    scores = jnp.where(admitted > 0.5, dot_nt(rows, tk_ref[0]) * scale, NEG)
    highest = jnp.max(scores, -1, keepdims=True)
    probs = jnp.exp2(scores - highest)
    m_ref[...] = jnp.broadcast_to(highest, m_ref.shape)
    l_ref[...] = jnp.broadcast_to(jnp.sum(probs, -1, keepdims=True), l_ref.shape)
    acc_ref[...] = dot_nn(probs.astype(BF16), tv_ref[0])

    length = len_ref[r]

    def step(start, chunk, masked):
        start = pl.multiple_of(start, chunk)
        s = dot_nt(rows, ck_ref[0, 0, pl.ds(start, chunk), :]) * scale
        if masked:
            place = lax.broadcasted_iota(jnp.int32, s.shape, 1)
            s = jnp.where(place < length - start, s, NEG)
        before = m_ref[:, :1]
        now = jnp.maximum(before, jnp.max(s, -1, keepdims=True))
        p = jnp.exp2(s - now)
        fade = jnp.exp2(before - now)
        l_ref[...] = l_ref[...] * fade + jnp.sum(p, -1, keepdims=True)
        acc_ref[...] = acc_ref[...] * fade + dot_nn(
            p.astype(BF16), cv_ref[0, 0, pl.ds(start, chunk), :]
        )
        m_ref[...] = jnp.broadcast_to(now, m_ref.shape)

    done = 0
    for chunk in CHUNKS:
        assert cache % chunk == 0
        upto = length // chunk

        @pl.loop(done // chunk, upto)
        def _(i, chunk=chunk):
            step(i * chunk, chunk, False)

        done = upto * chunk

    @pl.when(done < length)
    def _():
        step(done, CHUNKS[-1], True)

    o = (acc_ref[...] / l_ref[:, :1]).astype(BF16)
    for g in range(groups):
        attended[r, :, g * hd : (g + 1) * hd] = o[g * tree : (g + 1) * tree]

    @pl.when(r == last)
    def _():
        weights.wait()
        a = attended[...].reshape(-1, width)
        out_ref[...] = dot_nn(a, wo_ref[...]).astype(BF16)


def attend(queries, tree_keys, tree_values, cache_keys, cache_values, lengths, parents, out_weight):
    req, tree, width = queries.shape
    cache, hd = cache_keys.shape[2:]
    assert cache_keys.shape[1] == 1
    model = out_weight.shape[1]
    rows = tree * (width // hd)
    grid_spec = pltpu.PrefetchScalarGridSpec(
        num_scalar_prefetch=1,
        grid=(req,),
        in_specs=[
            pl.BlockSpec((1, tree, width), lambda r, n: (r, 0, 0)),
            pl.BlockSpec((1, tree, hd), lambda r, n: (r, 0, 0)),
            pl.BlockSpec((1, tree, hd), lambda r, n: (r, 0, 0)),
            pl.BlockSpec((1, 1, tree), lambda r, n: (r, 0, 0)),
            pl.BlockSpec((1, 1, cache, hd), lambda r, n: (r, 0, 0, 0)),
            pl.BlockSpec((1, 1, cache, hd), lambda r, n: (r, 0, 0, 0)),
            pl.BlockSpec(memory_space=pl.ANY),
        ],
        out_specs=pl.BlockSpec((req * tree, model), lambda r, n: (0, 0)),
        scratch_shapes=[
            pltpu.VMEM((req, tree, width), BF16),
            pltpu.VMEM((rows, LANES), F32),
            pltpu.VMEM((rows, LANES), F32),
            pltpu.VMEM((rows, hd), F32),
            pltpu.VMEM(out_weight.shape, BF16),
            pltpu.SemaphoreType.DMA,
        ],
    )
    return pl.pallas_call(
        attend_kernel,
        grid_spec=grid_spec,
        out_shape=jax.ShapeDtypeStruct((req * tree, model), BF16),
        compiler_params=pltpu.CompilerParams(
            dimension_semantics=("arbitrary",), vmem_limit_bytes=67043328
        ),
    )(lengths, queries, tree_keys, tree_values, parents.reshape(req, 1, tree), cache_keys,
      cache_values, out_weight)


def copy_count(z_n, y_n, x_n):
    gather = 2 * (z_n - 1) + z_n * (x_n * y_n - 1) * 2 + 2 * z_n * y_n * x_n
    back = 2 * z_n + 2 * z_n * (y_n - 1 + x_n - 1) + 2 * (z_n - 1)
    return (y_n * x_n - 1) + gather + back


def expert_kernel(
    dims, part_ref, hid_ref, gain_ref, ids_ref, rw_ref, gu_hbm, dn_hbm, out_ref,
    head_in, bank, sums, pair_in, first_in, second_in, z_in, resid_ref, gu, dn,
    send, recv, load_sem,
):
    z_n, y_n, x_n = dims
    h_n = y_n * x_n
    s = lax.axis_index("sec")
    z = lax.axis_index("req")
    h = lax.axis_index("head")
    y = h // x_n
    x = h % x_n
    tok, model = hid_ref.shape
    half = model // 2
    mine = (s * z_n + z) * h_n + h

    def to_head(k):
        return {"head": lax.rem(h + k, h_n)}

    def to_z(k):
        return {"req": lax.rem(z + k, z_n)}

    def to_yx(dy, dx):
        return {"head": lax.rem(y + dy, y_n) * x_n + lax.rem(x + dx, x_n)}

    partner = {"sec": 1 - s}
    barrier = pltpu.get_barrier_semaphore()
    peers = [to_head(k) for k in range(1, h_n)] + [to_z(k) for k in range(1, z_n)] + [partner]
    for peer in peers:
        pl.semaphore_signal(
            barrier, inc=1, device_id=peer, device_id_type=pl.DeviceIdType.MESH
        )
    load_gu = pltpu.make_async_copy(gu_hbm.at[0], gu, load_sem.at[0])
    load_dn = pltpu.make_async_copy(dn_hbm.at[0], dn, load_sem.at[1])
    load_gu.start()
    load_dn.start()
    pl.semaphore_wait(barrier, len(peers))

    made = []

    def push(src, dst, peer):
        k = len(made)
        c = pltpu.make_async_remote_copy(
            src_ref=src, dst_ref=dst, send_sem=send.at[k], recv_sem=recv.at[k],
            device_id=peer, device_id_type=pl.DeviceIdType.MESH,
        )
        made.append(c)
        c.start()
        return c

    arrivals = []
    for k in range(1, h_n):
        row = pl.multiple_of(lax.rem(h + k, h_n) * tok, tok)
        arrivals.append(push(part_ref.at[pl.ds(row, tok), :], head_in.at[k - 1], to_head(k)))
    lanes = bank.shape[-1] - half
    labels = lax.broadcasted_iota(jnp.int32, (lanes, tok), 0)
    dense = jnp.zeros((lanes, tok), F32)
    for k in range(ids_ref.shape[0]):
        dense = dense + jnp.where(ids_ref[k : k + 1, :] == labels, rw_ref[k : k + 1, :], 0.0)
    high = dense.astype(BF16)
    low = (dense - high.astype(F32)).astype(BF16)
    eye = (
        lax.broadcasted_iota(jnp.int32, (tok, tok), 0)
        == lax.broadcasted_iota(jnp.int32, (tok, tok), 1)
    ).astype(F32).astype(BF16)
    high = dot_nt(eye, high).astype(BF16)
    low = dot_nt(eye, low).astype(BF16)
    own_row = pl.multiple_of(h * tok, tok)
    resid = hid_ref[...].astype(F32) + part_ref[pl.ds(own_row, tok), :].astype(F32)
    for k in range(1, h_n):
        arrivals[k - 1].wait_recv()
        resid = resid + head_in[k - 1].astype(F32)
    resid_ref[...] = resid
    normed = (
        resid * lax.rsqrt(jnp.mean(resid * resid, -1, keepdims=True) + 1e-06) * gain_ref[...]
    ).astype(BF16)
    for f, extra in ((0, high), (1, low)):
        bank[0, f, 0, 0, 0, :, :half] = normed[:, f * half : (f + 1) * half]
        bank[0, f, 0, 0, 0, :, half:] = extra

    got = {}

    def gather(f, dz, dy, dx, src, peer):
        got[f, dz, dy, dx] = push(
            bank.at[(0, f, dz) + src], bank.at[0, f, dz, dy, dx], peer
        )

    for dz in range(1, z_n):
        for f in range(2):
            got[f, dz, 0, 0] = push(bank.at[0, f, 0, 0, 0], bank.at[0, f, dz, 0, 0], to_z(dz))

    crossed = {}

    def cross(f, dz, dy, dx):
        crossed[f, dz, dy, dx] = push(
            bank.at[0, f, dz, dy, dx], bank.at[1, f, dz, dy, dx], partner
        )

    def stage_a(dz):
        for f in range(2):
            if dz:
                got[f, dz, 0, 0].wait_recv()
            cross(f, dz, 0, 0)
            for dx in range(1, x_n):
                gather(f, dz, 0, dx, (0, 0), to_yx(0, dx)) if f == 0 else None
            for dy in range(1, y_n):
                gather(f, dz, dy, 0, (0, 0), to_yx(dy, 0)) if f == 1 else None
        for dy in range(1, y_n):
            gather(0, dz, dy, 0, (0, 0), to_yx(dy, 0))
        for dx in range(1, x_n):
            gather(1, dz, 0, dx, (0, 0), to_yx(0, dx))

    def stage_b(dz):
        for dx in range(1, x_n):
            got[0, dz, 0, dx].wait_recv()
            for dy in range(1, y_n):
                gather(0, dz, dy, dx, (0, dx), to_yx(dy, 0))
            cross(0, dz, 0, dx)
        for dy in range(1, y_n):
            got[1, dz, dy, 0].wait_recv()
            for dx in range(1, x_n):
                gather(1, dz, dy, dx, (dy, 0), to_yx(0, dx))
            cross(1, dz, dy, 0)

    def stage_c(dz):
        for f in range(2):
            for dy in range(y_n):
                for dx in range(x_n):
                    seen = (dy == 0 and dx == 0) or (f == 0 and dy == 0) or (f == 1 and dx == 0)
                    if not seen:
                        got[f, dz, dy, dx].wait_recv()
                        cross(f, dz, dy, dx)

    count = 2 * h_n * tok
    apart = 1 if h_n * tok <= 128 else y_n

    def experts(dz):
        for f in range(2):
            for dy in range(y_n):
                for dx in range(x_n):
                    crossed[f, dz, dy, dx].wait_recv()
        pick = lax.broadcasted_iota(jnp.int32, (1, lanes), 1) == mine
        for part in range(apart):
            ys = slice(part * (y_n // apart), (part + 1) * (y_n // apart))
            left = bank[:, 0, dz, ys].reshape(count // apart, half + lanes)
            right = bank[:, 1, dz, ys].reshape(count // apart, half + lanes)
            named = left[:, half:].astype(F32) + right[:, half:].astype(F32)
            weight = jnp.sum(jnp.where(pick, named, 0.0), -1, keepdims=True)
            mixed = dot_nn(left[:, :half], gu[:half]) + dot_nn(right[:, :half], gu[half:])
            hidden = mixed.shape[1] // 2
            gate = mixed[:, :hidden]
            active = (gate / (1.0 + jnp.exp(-gate)) * mixed[:, hidden:]).astype(BF16)
            result = jnp.where(weight > 0.0, dot_nn(active, dn[...]) * weight, 0.0).astype(BF16)
            shaped = result.reshape(2, y_n // apart, x_n, tok, model)
            for f in range(2):
                sums[f, dz, ys] = shaped[0, ..., f * half : (f + 1) * half]
                bank[1, f, dz, ys, :, :, :half] = shaped[1, ..., f * half : (f + 1) * half]

    paired, firsts, seconds, ends = {}, {}, {}, {}

    def back_pair(dz):
        for f in range(2):
            paired[f, dz] = push(
                bank.at[1, f, dz, :, :, :, pl.ds(0, half)], pair_in.at[f, dz], partner
            )

    def back_first(dz):
        for f in range(2):
            paired[f, dz].wait_recv()
            sums[f, dz] = (sums[f, dz].astype(F32) + pair_in[f, dz].astype(F32)).astype(BF16)
            if f == 0:
                for dy in range(1, y_n):
                    firsts[f, dz, dy] = push(
                        sums.at[f, dz, dy], first_in.at[f, dz, dy - 1], to_yx(y_n - dy, 0)
                    )
            else:
                for dx in range(1, x_n):
                    firsts[f, dz, dx] = push(
                        sums.at[f, dz, :, dx], first_in.at[f, dz, dx - 1], to_yx(0, x_n - dx)
                    )

    def back_second(dz):
        for f in range(2):
            total = sums[f, dz, 0] if f == 0 else sums[f, dz, :, 0]
            total = total.astype(F32)
            for d in range(1, y_n if f == 0 else x_n):
                firsts[f, dz, d].wait_recv()
                total = total + first_in[f, dz, d - 1].astype(F32)
            if f == 0:
                sums[f, dz, 0] = total.astype(BF16)
                for dx in range(1, x_n):
                    seconds[f, dz, dx] = push(
                        sums.at[f, dz, 0, dx], second_in.at[f, dz, dx - 1], to_yx(0, x_n - dx)
                    )
            else:
                sums[f, dz, :, 0] = total.astype(BF16)
                for dy in range(1, y_n):
                    seconds[f, dz, dy] = push(
                        sums.at[f, dz, dy, 0], second_in.at[f, dz, dy - 1], to_yx(y_n - dy, 0)
                    )

    def back_end(dz):
        for f in range(2):
            total = sums[f, dz, 0, 0].astype(F32)
            for d in range(1, x_n if f == 0 else y_n):
                seconds[f, dz, d].wait_recv()
                total = total + second_in[f, dz, d - 1].astype(F32)
            if dz:
                sums[f, dz, 0, 0] = total.astype(BF16)
                ends[f, dz] = push(sums.at[f, dz, 0, 0], z_in.at[f, dz - 1], to_z(z_n - dz))
            else:
                cols = slice(f * half, (f + 1) * half)
                resid_ref[:, cols] = resid_ref[:, cols] + total

    order = list(range(1, z_n)) + [0]

    def back(j):
        for stage, lag in ((back_end, 3), (back_second, 2), (back_first, 1)):
            if 0 <= j - lag < z_n:
                stage(order[j - lag])

    ran = 0
    for i in range(z_n + 2):
        for stage, lag in ((stage_a, 0), (stage_b, 1), (stage_c, 2)):
            if 0 <= i - lag < z_n:
                stage(i - lag)
        if i == 2:
            load_gu.wait()
            load_dn.wait()
        while ran < z_n and (i == z_n + 1 or order[ran] <= i - 2 and order[ran] > 0):
            experts(order[ran])
            back_pair(order[ran])
            back(ran)
            ran += 1
    for j in range(z_n, z_n + 3):
        back(j)
    for f in range(2):
        cols = slice(f * half, (f + 1) * half)
        total = resid_ref[:, cols]
        for dz in range(1, z_n):
            ends[f, dz].wait_recv()
            total = total + z_in[f, dz - 1].astype(F32)
        out_ref[:, cols] = total.astype(BF16)
    for c in made:
        c.wait_send()
    assert len(made) == copy_count(*dims)


def expert_layer(dims, partial, hidden, gain, ids, route, gate_up, down):
    z_n, y_n, x_n = dims
    tok, model = hidden.shape
    half = model // 2
    experts = gate_up.shape[0] * 2 * z_n * y_n * x_n
    assert gate_up.shape[0] == 1 and partial.shape[0] == y_n * x_n * tok
    lanes = -(-experts // LANES) * LANES
    most = max(y_n, x_n)
    copies = copy_count(*dims)
    vmem = pl.BlockSpec(memory_space=pltpu.VMEM)
    return pl.pallas_call(
        functools.partial(expert_kernel, dims),
        out_shape=jax.ShapeDtypeStruct((tok, model), BF16),
        in_specs=[vmem] * 5 + [pl.BlockSpec(memory_space=pl.ANY)] * 2,
        out_specs=vmem,
        scratch_shapes=[
            pltpu.VMEM((y_n * x_n - 1, tok, model), BF16),
            pltpu.VMEM((2, 2, z_n, y_n, x_n, tok, half + lanes), BF16),
            pltpu.VMEM((2, z_n, y_n, x_n, tok, half), BF16),
            pltpu.VMEM((2, z_n, y_n, x_n, tok, half), BF16),
            pltpu.VMEM((2, z_n, most - 1, most, tok, half), BF16),
            pltpu.VMEM((2, z_n, most - 1, tok, half), BF16),
            pltpu.VMEM((2, z_n - 1, tok, half), BF16),
            pltpu.VMEM((tok, model), F32),
            pltpu.VMEM(gate_up.shape[1:], BF16),
            pltpu.VMEM(down.shape[1:], BF16),
            pltpu.SemaphoreType.DMA((copies,)),
            pltpu.SemaphoreType.DMA((copies,)),
            pltpu.SemaphoreType.DMA((2,)),
        ],
        compiler_params=pltpu.CompilerParams(
            collective_id=0, has_side_effects=True, vmem_limit_bytes=67043328
        ),
    )(partial, hidden, gain.reshape(1, -1), ids.T, route.T, gate_up, down)


def per_device(
    dims, queries, tree_keys, tree_values, cache_keys, cache_values, cache_lengths, tree_parents,
    out_weight, hidden, norm_gain, expert_ids, route_weights, expert_gate_up, expert_down,
):
    partial = attend(
        queries, tree_keys, tree_values, cache_keys, cache_values, cache_lengths, tree_parents,
        out_weight,
    )
    return expert_layer(
        dims, partial, hidden, norm_gain, expert_ids, route_weights, expert_gate_up, expert_down
    )


def solution(mesh):
    heads = mesh.shape["head"]
    x_n = math.isqrt(heads)
    while heads % x_n:
        x_n -= 1
    assert mesh.shape["sec"] == 2
    dims = (mesh.shape["req"], heads // x_n, x_n)
    tokens = ("sec", "req", "head")
    in_specs = (
        P(("sec", "req"), None, "head"),
        P(("sec", "req"), None, "head"),
        P(("sec", "req"), None, "head"),
        P(("sec", "req"), "head", None, None),
        P(("sec", "req"), "head", None, None),
        P(("sec", "req")),
        P(("sec", "req"), None),
        P("head", None),
        P(tokens, None),
        P(),
        P(tokens, None),
        P(tokens, None),
        P(tokens, None, None),
        P(tokens, None, None),
    )
    return jax.shard_map(
        functools.partial(per_device, dims), mesh=mesh, in_specs=in_specs,
        out_specs=P(tokens, None), check_vma=False,
    )
```
